256 devices in a mesh: seq: 64 (over y, x, z_hi, core), tp: 4 (over z_lo).
Axes of the slice: x: 4, y: 4, z: 8 (z_hi: 2, z_lo: 4; z = z_hi * 4 + z_lo), core: 2. Of those that a mesh axis runs over, the one named last changes fastest.
Arguments:
- tokens: bfloat16 [32768, 2048], P('seq'), may hold values from -6 to 6
- norm_gain: float32 [2048], replicated, may hold values from 0.1 to 1.9
- query_key_value_weight: bfloat16 [2048, 8, 384], P(None, 'tp'), may hold values from -8 to 8
- output_weight: bfloat16 [8, 256, 2048], P('tp'), may hold values from -0.75 to 0.75
- out_gain: float32 [2048], P('tp'), may hold values from 0.1 to 1.9
- seg_ids: int32 [32768], P('seq'), may hold values from 0 to 15, never falling along the last dimension, each value on 1 to 8192 neighbouring positions
- earlier_cache: bfloat16 [4096, 8, 2048], P('seq', 'tp'), may hold values from -6 to 6
- decode_owner: int32 [4096, 1], P('seq'), may hold values from 0 to 63; in each aligned block of 64 rows (0 to 63, 64 to 127, ...) at most 2 rows name the same one
Outputs:
- hidden_out: bfloat16 [32768, 2048], P('seq', 'tp')
- mlp_input: bfloat16 [32768, 2048], P('seq', 'tp')
- decode_layout_cache: bfloat16 [8192, 8, 2048], P('seq', 'tp')
The draws below stay inside these ranges and needn't reach their ends.
Inputs may be any that keep to these rules, and one draw needn't show every extreme that they name: `seg_ids`: request ids never fall along the tokens; every request 0 to 15 holds 1 to 8192 tokens in a row, and one holds exactly 8192. `decode_owner`: among the 64 rows of one device (aligned blocks of 64 rows) no owner is named more than 2 times; some owner is named exactly 2 times in some block.
All inputs are finite; a program needn't handle non-finite values.
Results may differ from the reference program's by a relative error of at most 0.014.
The reference program's roundings to bfloat16 on the way count: a program that leaves them out, or rounds other values in their place, can miss the bound.
Values may be sent and summed in bfloat16 or wider, within the bound.
A program may use at most 64 MiB of HBM per device.

```python
import math
import jax
import jax.numpy as jnp
import numpy as np
from jax import lax

MODEL_DIM = 2048
HQ = 32
KEY_VALUE_HEADS = 8
HEAD_SIZE = 64
QUERY_PER_KEY = 4
REQS = 16
BLOCK_TOKENS = 16
PB = 64
STRETCH_TOKENS = 32768
PRIOR_BLOCKS = 4096
MOST = 2
DECODE_CACHE_SLOTS = 8192
N_SEQ = 64


def draw_query_key_value_weight(key, part):
    leading_key = jax.random.fold_in(jax.random.fold_in(key, 17), 0)
    entry_scaling = MODEL_DIM ** (-0.5)
    cache_entries = jnp.clip(jax.random.normal(leading_key, (MODEL_DIM, KEY_VALUE_HEADS, QUERY_PER_KEY + 2, HEAD_SIZE), jnp.float32), -6.0, 6.0) * entry_scaling
    return jnp.clip(cache_entries, -8.0, 8.0).reshape(MODEL_DIM, KEY_VALUE_HEADS, (QUERY_PER_KEY + 2) * HEAD_SIZE).astype(jnp.bfloat16)


def block_scale(rng, shape, cuts, least, high):
    def one(axis_at, blocks):
        steps = jax.random.uniform(jax.random.fold_in(jax.random.fold_in(rng, 6), axis_at), (blocks,), jnp.float32, least / len(cuts), high / len(cuts))
        return jnp.repeat(jnp.exp(steps), shape[axis_at] // blocks).reshape((-1,) + (1,) * (len(shape) - axis_at - 1))

    level = one(*cuts[0])
    for cut in cuts[1:]:
        level = level * one(*cut)
    return level


def profile(count, total, bound, slope):
    portions = [(1 << 20) // math.isqrt(grade ** slope) + 1 for grade in range(2, count + 1)]
    spare, given = total - bound - (count - 1), [1] * (count - 1)
    while spare > 0:
        free = [i for i in range(count - 1) if given[i] < bound]
        pool, budget = sum([portions[i] for i in free]), spare
        for i in free:
            addition = min(bound - given[i], max(1, budget * portions[i] // pool), spare)
            given[i] = given[i] + addition
            spare = spare - addition
    return np.array([bound] + given)


def ragged(stream_key, amount, total, most, slope):
    if amount == 2:
        one = jax.random.randint(stream_key, (), max(1, total - most), min(most, total - 1) + 1)
        return jnp.stack([one, total - one])
    lengths = jnp.asarray(profile(amount, total, most, slope), jnp.int32)
    pairs = (amount - 1) // 2
    giver, sink = lengths[1:1 + 2 * pairs:2], lengths[2:2 + 2 * pairs:2]
    slack = jnp.minimum(giver - 1, most - sink)
    moved = jax.random.randint(jax.random.fold_in(stream_key, 1), (pairs,), 0, 1 << 20) % (slack + 1)
    lengths = lengths.at[1:1 + 2 * pairs:2].set(giver - moved).at[2:2 + 2 * pairs:2].set(sink + moved)
    return lengths[jax.random.permutation(jax.random.fold_in(stream_key, 2), amount)]


def shared_out(own_key, own, number, rows, count, top, bound, slope):
    order = jax.random.permutation(own_key, count)
    heavy_load, ordinary = shares(count, rows * top, bound, slope, True), shares(count, rows * top, bound, slope, False)
    places = jnp.arange(count)

    def named(sizes, turn):
        used = int((sizes > 0).sum())
        fixed = max(1, used // 4)
        moved = fixed + (places - fixed + turn * (used - fixed)) % max(1, count - fixed)
        return jnp.zeros((count,), jnp.int32).at[order[jnp.where(places < fixed, places, moved)]].set(jnp.asarray(sizes, jnp.int32))

    sizes = jnp.where(number % 4 == 0, named(heavy_load, number // 4), named(ordinary, number - number // 4 - 1))
    mixed = jax.random.permutation(jax.random.fold_in(own, 3), count)
    source_of, receiver = mixed[0:count // 2 * 2:2], mixed[1:count // 2 * 2:2]
    margin = jnp.minimum(sizes[source_of] - 1, bound - sizes[receiver]) // 2
    margin = jnp.where((source_of == order[0]) | (receiver == order[0]) | (sizes[receiver] == 0), 0, jnp.maximum(margin, 0))
    moved = jax.random.randint(jax.random.fold_in(own, 4), (count // 2,), 0, 1 << 20) % (margin + 1)
    sizes = sizes.at[source_of].add(-moved).at[receiver].add(moved)
    members = jnp.searchsorted(jnp.cumsum(sizes), jnp.arange(rows * top), side="right").astype(jnp.int32)
    table = members.reshape(top, rows).T
    table = table[jax.random.permutation(jax.random.fold_in(own, 1), rows)]
    turn = jax.random.randint(jax.random.fold_in(own, 2), (rows, 1), 0, top)
    return jnp.take_along_axis(table, (jnp.arange(top)[None, :] + turn) % top, axis=1)


def shares(count, total, most, lean, full):
    portions = [(1 << 20) // math.isqrt(rank ** lean) + 1 for rank in range(1, count + 1)]
    largest = most if full else min(most, max(-(-total // count), total * portions[0] // sum(portions)))
    least = 1 if total - largest >= count - 1 else 0
    holding, surplus = [largest] + [least] * (count - 1), total - largest - least * (count - 1)
    while surplus > 0:
        free = [i for i in range(1, count) if holding[i] < largest] or [i for i in range(1, count) if holding[i] < most]
        pool, budget = sum([portions[i] for i in free]), surplus
        for i in free:
            extra = min(most - holding[i], max(1, budget * portions[i] // pool), surplus)
            holding[i] = holding[i] + extra
            surplus = surplus - extra
    return np.array(holding)


def centred(own_key, shape, deviation, most, shards=(), held_as=jnp.bfloat16):
    loudness = block_scale(own_key, shape, shards, -0.22, 0.18) if shards else 1.0
    values = jax.random.normal(own_key, shape, jnp.float32) * deviation * loudness
    return jnp.minimum(jnp.maximum(values, -most), most).astype(held_as)


def setup_inputs(seed: int = 0) -> dict:
    keys = jax.random.split(jax.random.key(seed), 9)
    tokens = centred(keys[0], (STRETCH_TOKENS, MODEL_DIM), 1.0, 6.0, ((0, 64),))
    norm_gain = jnp.clip(1.0 + 0.18 * jax.random.normal(keys[1], (MODEL_DIM,), jnp.float32), 0.1, 1.9)
    query_key_value_weight = draw_query_key_value_weight(jax.random.fold_in(keys[8], 71), 0)
    output_weight = centred(keys[3], (KEY_VALUE_HEADS, QUERY_PER_KEY * HEAD_SIZE, MODEL_DIM), HEAD_SIZE ** -0.5, 0.75, ((0, 4),))
    out_gain = jnp.clip(1.0 + 0.18 * jax.random.normal(keys[4], (MODEL_DIM,), jnp.float32), 0.1, 1.9)
    seg_ids = jnp.searchsorted(jnp.cumsum(ragged(keys[5], REQS, STRETCH_TOKENS, STRETCH_TOKENS // 4, 2)), jnp.arange(STRETCH_TOKENS), side="right").astype(jnp.int32)
    earlier_cache = centred(keys[6], (PRIOR_BLOCKS, KEY_VALUE_HEADS, 2 * BLOCK_TOKENS * HEAD_SIZE), 1.0, 6.0, ((0, 64), (1, 4)))
    decode_owner_keys = jax.random.split(jax.random.fold_in(keys[7], 1), PRIOR_BLOCKS // PB)
    decode_owner_turns = jax.random.permutation(jax.random.fold_in(keys[7], 3), PRIOR_BLOCKS // PB)
    decode_owner = jax.vmap(lambda own, number: shared_out(jax.random.fold_in(keys[7], 2), own, number, PB, N_SEQ, 1, MOST, 1))(decode_owner_keys, decode_owner_turns).reshape((PRIOR_BLOCKS, 1))
    return dict(tokens=tokens, norm_gain=norm_gain, query_key_value_weight=query_key_value_weight, output_weight=output_weight, out_gain=out_gain, seg_ids=seg_ids, earlier_cache=earlier_cache, decode_owner=decode_owner)


def norm_scale(cache_entries, gain_row):
    mean_square = lax.optimization_barrier(jnp.mean(cache_entries * cache_entries, axis=-1, keepdims=True))
    return cache_entries * lax.rsqrt(mean_square + 1e-05) * gain_row

def angles(position, head_dim):
    half_dim = head_dim // 2
    frequency = jnp.exp(-(2.0 * jnp.arange(half_dim, dtype=jnp.float32) / head_dim) * math.log(500000.0))
    return position.astype(jnp.float32)[:, None] * frequency[None, :]

def apply_rotary(cache_entries, rotary_phase):
    half_dim = cache_entries.shape[-1] // 2
    cosine = jnp.cos(rotary_phase)[:, None, :]
    sine_part = jnp.sin(rotary_phase)[:, None, :]
    first_half = cache_entries[..., :half_dim]
    second_half = cache_entries[..., half_dim:]
    return jnp.concatenate([first_half * cosine - second_half * sine_part, second_half * cosine + first_half * sine_part], axis=-1)

def reference(tokens, norm_gain, query_key_value_weight, output_weight, out_gain, seg_ids, earlier_cache, decode_owner):
    values_in = tokens.astype(jnp.float32)
    normalized_input = norm_scale(values_in, norm_gain).astype(jnp.bfloat16)
    projected_rows = jnp.dot(normalized_input, query_key_value_weight.reshape(MODEL_DIM, KEY_VALUE_HEADS * (QUERY_PER_KEY + 2) * HEAD_SIZE), preferred_element_type=jnp.float32)
    projected_rows = projected_rows.reshape(STRETCH_TOKENS, KEY_VALUE_HEADS, QUERY_PER_KEY + 2, HEAD_SIZE)
    token_index = jnp.arange(STRETCH_TOKENS, dtype=jnp.int32)
    request = jnp.arange(REQS, dtype=jnp.int32)
    member = seg_ids[:, None] == request[None, :]
    request_first = lax.optimization_barrier(jnp.min(jnp.where(member, token_index[:, None], STRETCH_TOKENS), axis=0))
    position = token_index - lax.optimization_barrier(jnp.sum(jnp.where(member, request_first[None, :], 0), axis=1))
    rotary_phase = angles(position, HEAD_SIZE)
    query_rows = apply_rotary(projected_rows[:, :, :QUERY_PER_KEY].reshape(STRETCH_TOKENS, KEY_VALUE_HEADS * QUERY_PER_KEY, HEAD_SIZE), rotary_phase) * HEAD_SIZE ** (-0.5)
    query_rows = query_rows.astype(jnp.bfloat16).reshape(STRETCH_TOKENS, KEY_VALUE_HEADS, QUERY_PER_KEY, HEAD_SIZE)
    key_rows = apply_rotary(projected_rows[:, :, QUERY_PER_KEY], rotary_phase).astype(jnp.bfloat16)
    values = projected_rows[:, :, QUERY_PER_KEY + 1].astype(jnp.bfloat16)
    query_rows, key_rows, values = lax.optimization_barrier((query_rows, key_rows, values))
    block_rows = math.gcd(STRETCH_TOKENS, 512)
    key_span = min(STRETCH_TOKENS, STRETCH_TOKENS // 4 + block_rows)

    def attend(block_index):
        query_start = block_index * block_rows
        key_start = jnp.maximum(query_start + block_rows - key_span, 0).astype(jnp.int32)
        query_block = lax.dynamic_slice_in_dim(query_rows, query_start, block_rows, 0).astype(jnp.float32)
        key_block = lax.dynamic_slice_in_dim(key_rows, key_start, key_span, 0).astype(jnp.float32)
        value_block = lax.dynamic_slice_in_dim(values, key_start, key_span, 0).astype(jnp.float32)
        query_seg = lax.dynamic_slice_in_dim(seg_ids, query_start, block_rows, 0)
        key_seg = lax.dynamic_slice_in_dim(seg_ids, key_start, key_span, 0)
        query_pos = query_start + jnp.arange(block_rows, dtype=jnp.int32)
        key_pos = key_start + jnp.arange(key_span, dtype=jnp.int32)
        scores = jnp.einsum('qhgd,khd->hgqk', query_block, key_block)
        allowed = (query_seg[:, None] == key_seg[None, :]) & (key_pos[None, :] <= query_pos[:, None])
        scores = jnp.where(allowed, scores, -1e+30)
        row_max = lax.optimization_barrier(jnp.max(scores, axis=-1, keepdims=True))
        weights = jnp.where(allowed, jnp.exp(scores - row_max), 0.0)
        denominator = lax.optimization_barrier(jnp.sum(weights, axis=-1))
        rounded_weights = lax.optimization_barrier(weights.astype(jnp.bfloat16))
        summed = jnp.einsum('hgqk,khd->qhgd', rounded_weights.astype(jnp.float32), value_block)
        attended_block = summed / jnp.transpose(denominator, (2, 0, 1))[..., None]
        return attended_block.astype(jnp.bfloat16)
    attended = lax.map(attend, jnp.arange(STRETCH_TOKENS // block_rows, dtype=jnp.int32))
    attended = attended.reshape(STRETCH_TOKENS, HQ * HEAD_SIZE)
    projected_out = jnp.dot(attended, output_weight.reshape(HQ * HEAD_SIZE, MODEL_DIM), preferred_element_type=jnp.float32)
    residual = values_in + projected_out
    hidden_out = residual.astype(jnp.bfloat16)
    mlp_input = norm_scale(residual, out_gain).astype(jnp.bfloat16)
    owner_index = decode_owner[:, 0]
    grouped = owner_index.reshape(N_SEQ, PB)
    owner_hits = (grouped[:, :, None] == jnp.arange(N_SEQ, dtype=jnp.int32)[None, None, :]).astype(jnp.int32)
    slot_rank = lax.optimization_barrier(jnp.sum((jnp.cumsum(owner_hits, axis=1) - 1) * owner_hits, axis=2)).reshape(PRIOR_BLOCKS)
    source = jnp.arange(PRIOR_BLOCKS, dtype=jnp.int32) // PB
    decode_slot_row = (owner_index * (2 * PB) + source * MOST + slot_rank).astype(jnp.int32)
    decode_layout_cache = jnp.zeros((DECODE_CACHE_SLOTS, KEY_VALUE_HEADS, 2 * BLOCK_TOKENS * HEAD_SIZE), jnp.bfloat16).at[decode_slot_row].set(earlier_cache)
    return (hidden_out, mlp_input, decode_layout_cache)
```

```python
import functools
import math

import jax
import jax.numpy as jnp
import numpy as np
from jax import lax
from jax.experimental import pallas as pl
from jax.experimental.pallas import tpu as pltpu
from jax.sharding import PartitionSpec as P

HEAD_SIZE = 64
QUERY_PER_KEY = 4
REQS = 16
BIG = float(2.0**100)
CHUNKS = 4
PACKET_ROWS = 512 + 4 * 144
PAIRS = 8
EARLY_PAIRS = 5
MESH = pl.DeviceIdType.MESH
F32 = jnp.float32
BF16 = jnp.bfloat16


def rope_tables(tok, blocks):
    half = HEAD_SIZE // 2
    freq = 500000.0 ** (-2.0 * np.arange(half) / HEAD_SIZE)
    inner = freq[:, None] * np.arange(tok)[None, :]
    outer = freq[:, None] * (np.arange(128) * tok)[None, :]
    parts = [np.cos(inner), np.sin(inner), np.cos(outer), np.sin(outer)]
    return np.concatenate(parts, axis=1).astype(np.float32)


def body(
    n_seq,
    n_tp,
    x_hbm,
    gain_ref,
    w_hbm,
    wo_hbm,
    ogain_ref,
    seg_ref,
    cache_hbm,
    inv_ref,
    rope_ref,
    hid_ref,
    mlp_ref,
    dec_hbm,
    xv,
    wv,
    wov,
    cachev,
    outg,
    kvb,
    kf,
    qt,
    mx,
    acc,
    resid,
    rs_send,
    rs_recv,
    ss_send,
    ss_recv,
    lsem,
    c_ssem,
    c_rsem,
    kv_ssem,
    kv_rsem,
    r_ssem,
    r_rsem,
    s_ssem,
    s_rsem,
):
    me = lax.axis_index("seq")
    tp = lax.axis_index("tp")
    core = lax.rem(me, 2)
    zh = lax.rem(me // 2, 2)
    xx = lax.rem(me // 4, 4)
    slab = (me // 16) * 16
    tok = 512

    cp_cache = pltpu.make_async_copy(cache_hbm, cachev.at[pl.ds(0, 64)], lsem.at[0])
    cp_x = pltpu.make_async_copy(x_hbm, xv, lsem.at[1])
    cp_w = pltpu.make_async_copy(w_hbm, wv, lsem.at[2])
    cp_wo = pltpu.make_async_copy(wo_hbm, wov, lsem.at[3])
    cp_cache.start()
    cp_x.start()
    cp_w.start()
    cp_wo.start()

    barrier = pltpu.get_barrier_semaphore()

    def greet(k, carry):
        pl.semaphore_signal(
            barrier,
            inc=1,
            device_id={"seq": lax.rem(me + k, n_seq), "tp": tp},
            device_id_type=MESH,
        )
        return carry

    lax.fori_loop(1, n_seq, greet, 0)
    for k in range(1, n_tp):
        pl.semaphore_signal(
            barrier,
            inc=1,
            device_id={"seq": me, "tp": lax.rem(tp + k, n_tp)},
            device_id_type=MESH,
        )

    cachev[64] = jnp.zeros((2, 2048), BF16)
    cp_cache.wait()

    def place(r, carry):
        outg[r] = cachev[inv_ref[r]]
        return carry

    lax.fori_loop(0, 2 * n_seq, place, 0)
    pl.semaphore_wait(barrier, n_seq - 1 + n_tp - 1)

    def cache_copy(k):
        to = lax.rem(me + k, n_seq)
        return pltpu.make_async_remote_copy(
            src_ref=outg.at[pl.ds(2 * to, 2)],
            dst_ref=dec_hbm.at[pl.ds(2 * me, 2)],
            send_sem=c_ssem.at[k],
            recv_sem=c_rsem.at[k],
            device_id={"seq": to, "tp": tp},
            device_id_type=MESH,
        )

    def cache_start(k, carry):
        cache_copy(k).start()
        return carry

    lax.fori_loop(1, n_seq, cache_start, 0)
    cp_own = pltpu.make_async_copy(
        outg.at[pl.ds(2 * me, 2)], dec_hbm.at[pl.ds(2 * me, 2)], lsem.at[4]
    )
    cp_own.start()

    lane = lax.broadcasted_iota(jnp.int32, (32, 128), 1)
    here = lane == me
    cos_b = jnp.sum(jnp.where(here, rope_ref[:, 2 * tok : 2 * tok + 128], 0.0), axis=1, keepdims=True)
    sin_b = jnp.sum(
        jnp.where(here, rope_ref[:, 2 * tok + 128 : 2 * tok + 256], 0.0), axis=1, keepdims=True
    )
    q_scale = HEAD_SIZE ** (-0.5) * math.log2(math.e)

    seg = seg_ref[...].astype(F32)
    seg0 = jnp.min(seg, axis=1, keepdims=True)
    carried_in = seg == seg0
    first = jnp.zeros((1, tok), F32)
    for r in range(1, REQS):
        below = jnp.sum(jnp.where(seg < r, 1.0, 0.0), axis=1, keepdims=True)
        first = jnp.where(seg == r, below, first)
    a_bias = jnp.where(carried_in, 0.0, -BIG)

    row16 = lax.broadcasted_iota(jnp.int32, (16, 512), 0)
    for c in range(CHUNKS):
        ab = a_bias[:, c * 128 : (c + 1) * 128]
        ab4 = jnp.concatenate([ab, ab, ab, ab], axis=1)
        feat = jnp.where(row16 == 0, ab4, jnp.where(row16 == 1, 1.0, 0.0)).astype(BF16)
        for kv in range(2):
            at = kv * 2048 + c * 512
            qt[128:144, at : at + 512] = feat
            qt[144:256, at : at + 512] = jnp.zeros((112, 512), BF16)
            qt[(1 - kv) * 64 : (1 - kv) * 64 + 64, at : at + 512] = jnp.zeros((64, 512), BF16)

    cp_x.wait()
    cp_w.wait()
    gain = gain_ref[...]
    aux_row = lax.broadcasted_iota(jnp.int32, (16, 128), 0)
    for c in range(CHUNKS):
        cols = slice(c * 128, (c + 1) * 128)
        xc = xv[cols, :].astype(F32)
        ms = jnp.mean(xc * xc, axis=1, keepdims=True)
        normed = (xc * lax.rsqrt(ms + 1e-05) * gain).astype(BF16)
        proj = jnp.dot(normed, wv[...], preferred_element_type=F32)
        ci = rope_ref[:, c * 128 : (c + 1) * 128]
        si = rope_ref[:, tok + c * 128 : tok + (c + 1) * 128]
        cos = ci * cos_b - si * sin_b
        sin = si * cos_b + ci * sin_b
        cos_q, sin_q = cos * q_scale, sin * q_scale

        def rot(a, co, sn):
            a1, a2 = a[0:32], a[32:64]
            return jnp.concatenate([a1 * co - a2 * sn, a2 * co + a1 * sn], axis=0)

        keys, vals = [], []
        for kv in range(2):
            for pair in range(2):
                at = kv * 384 + pair * 128
                tr = jnp.transpose(proj[:, at : at + 128])
                for g2 in range(2):
                    g = pair * 2 + g2
                    lane0 = kv * 2048 + c * 512 + g * 128
                    qt[kv * 64 : kv * 64 + 64, lane0 : lane0 + 128] = rot(
                        tr[g2 * 64 : g2 * 64 + 64], cos_q, sin_q
                    ).astype(BF16)
            tr = jnp.transpose(proj[:, kv * 384 + 256 : kv * 384 + 384])
            keys.append(rot(tr[0:64], cos, sin))
            vals.append(tr[64:128].astype(BF16))
        kvb[0, c * 128 : (c + 1) * 128, :] = jnp.transpose(
            jnp.concatenate(keys, axis=0)
        ).astype(BF16)
        aux = jnp.where(
            aux_row == 0, 1.0, jnp.where(aux_row == 1, seg[:, c * 128 : (c + 1) * 128], 0.0)
        ).astype(BF16)
        base = 512 + c * 144
        kvb[0, base : base + 64, :] = vals[0]
        kvb[0, base + 64 : base + 80, :] = aux
        kvb[0, base + 80 : base + 144, :] = vals[1]

    def packet(src, dst, sem, seq_to):
        return pltpu.make_async_remote_copy(
            src_ref=kvb.at[src],
            dst_ref=kvb.at[dst],
            send_sem=kv_ssem.at[sem],
            recv_sem=kv_rsem.at[dst],
            device_id={"seq": seq_to, "tp": tp},
            device_id_type=MESH,
        )

    a1 = jnp.where(zh == 1, 9, 17)
    b1 = jnp.where(zh == 1, 17, 9)
    z_to = me + 2 - 4 * zh
    y_to = lax.rem(me + 16, n_seq)
    sib = me + 1 - 2 * core

    def x_to(j):
        return slab + lax.rem(me - slab + 16 - 4 * j, 16)

    def x_src(j, a, b):
        dest_x = lax.rem(xx + 4 - j, 4)
        return jnp.where(dest_x > xx, a, b)

    copy_z = packet(0, jnp.where(zh == 0, 9, 17), 0, z_to)
    copy_y0 = packet(0, 1, 1, y_to)
    copy_y1 = packet(a1, b1, 2, y_to)
    copies_x0 = [packet(x_src(j, 0, 1), 2 + j, 2 + j, x_to(j)) for j in (1, 2, 3)]
    copies_x1 = [packet(x_src(j, a1, b1), 10 + j, 5 + j, x_to(j)) for j in (1, 2, 3)]
    copy_c0 = packet(jnp.where(core == 0, 0, 1), 2, 9, sib)
    copy_c1 = packet(9, 10, 10, sib)
    copies_f0 = [packet(2 + j, 5 + j, 10 + j, sib) for j in (1, 2, 3)]
    copies_f1 = [packet(10 + j, 13 + j, 13 + j, sib) for j in (1, 2, 3)]

    def arrived(slot):
        pltpu.make_async_copy(kvb.at[slot], kvb.at[slot], kv_rsem.at[slot]).wait()

    copy_y0.start()
    copy_z.start()

    def values_of(slot, kv):
        lo = 0 if kv == 0 else 64
        return jnp.concatenate(
            [kvb[slot, 512 + j * 144 + lo : 512 + j * 144 + lo + 80, :] for j in range(4)], axis=1
        )

    for c in range(CHUNKS):
        span = (c + 1) * 128
        key_at = lax.broadcasted_iota(jnp.int32, (span, 128), 0).astype(F32)
        query_at = lax.broadcasted_iota(jnp.int32, (span, 128), 1).astype(F32) + c * 128
        allowed1 = (key_at <= query_at) & (key_at >= first[:, c * 128 : (c + 1) * 128])
        bias1 = jnp.where(allowed1, 0.0, -BIG)
        bias = jnp.concatenate([bias1, bias1, bias1, bias1], axis=1)
        for kv in range(2):
            lanes = slice(kv * 2048 + c * 512, kv * 2048 + c * 512 + 512)
            s = jnp.dot(kvb[0, 0:span, :], qt[0:128, lanes], preferred_element_type=F32) + bias
            top = jnp.max(s, axis=0, keepdims=True)
            p = jnp.exp2(s - top).astype(BF16)
            mx[:, lanes] = jnp.broadcast_to(top, (8, 512))
            acc[:, lanes] = jnp.dot(
                values_of(0, kv)[:, 0:span], p, preferred_element_type=F32
            )

    u_at = lax.broadcasted_iota(jnp.int32, (512, 128), 0).astype(F32)
    f_lane = lax.broadcasted_iota(jnp.int32, (512, 128), 1)

    def prepare(slot):
        strange = jnp.zeros((1, 128), F32)
        for j in range(4):
            aux = kvb[slot, 512 + j * 144 + 64 : 512 + j * 144 + 80, :].astype(F32)
            strange = strange + jnp.where(aux[1:2, :] != seg0, 1.0, 0.0)
        count = jnp.sum(strange, axis=1, keepdims=True)
        bias = jnp.where(u_at < count, -BIG, 0.0)
        kf[slot] = jnp.where(f_lane == 0, 1.0, jnp.where(f_lane == 1, bias, 0.0)).astype(BF16)

    def unit(slot, kv, start, width):
        lanes = pl.ds(start, width)
        q = qt[:, lanes]
        scores = []
        for s in (slot, slot + 1):
            k = jnp.concatenate([kvb[s, 0:512, :], kf[s]], axis=1)
            scores.append(jnp.dot(k, q, preferred_element_type=F32))
        old = mx[:, lanes]
        tops = [jnp.max(s, axis=0, keepdims=True) for s in scores]
        new = jnp.maximum(old, jnp.maximum(tops[0], tops[1]))
        factor = jnp.exp2(old - new)
        total = acc[:, lanes] * factor[0:1]
        for i, s in enumerate(scores):
            p = jnp.exp2(s - new[0:1]).astype(BF16)
            total = total + jnp.dot(values_of(slot + i, kv), p, preferred_element_type=F32)
        acc[:, lanes] = total
        mx[:, lanes] = new

    def arrive(i):
        first_slot = 2 * i + 1

        @pl.when(i == 0)
        def _():
            arrived(1)
            for copy in copies_x0:
                copy.start()
            copy_c0.start()

        @pl.when(i == 1)
        def _():
            arrived(a1)
            copy_y1.start()

        @pl.when(i == 2)
        def _():
            arrived(b1)
            for copy in copies_x1:
                copy.start()
            copy_c1.start()

        for j in range(2):
            slot = first_slot + j

            @pl.when((slot != 1) & (slot != 9))
            def _():
                arrived(slot)

            @pl.when(((slot >= 3) & (slot <= 5)) | ((slot >= 11) & (slot <= 13)))
            def _():
                late = jnp.where(slot >= 11, 1, 0)
                packet(slot, slot + 3, slot + 8 - 5 * late, sib).start()

            prepare(slot)

    def early(i, carry):
        arrive(i)
        for kv in range(2):
            unit(2 * i + 1, kv, kv * 2048, 2048)
        return carry

    lax.fori_loop(0, EARLY_PAIRS, early, 0)

    cp_wo.wait()

    def reduce_copy(c, k):
        return pltpu.make_async_remote_copy(
            src_ref=rs_send.at[c, k - 1],
            dst_ref=rs_recv.at[c, k - 1],
            send_sem=r_ssem.at[c, k - 1],
            recv_sem=r_rsem.at[c, k - 1],
            device_id={"seq": me, "tp": lax.rem(tp + k, n_tp)},
            device_id_type=MESH,
        )

    def square_copy(c, k):
        return pltpu.make_async_remote_copy(
            src_ref=ss_send.at[c],
            dst_ref=ss_recv.at[c, k - 1],
            send_sem=s_ssem.at[c, k - 1],
            recv_sem=s_rsem.at[c, k - 1],
            device_id={"seq": me, "tp": lax.rem(tp + k, n_tp)},
            device_id_type=MESH,
        )

    def late(c, carry):
        def step(i, inner):
            @pl.when(c == 0)
            def _():
                arrive(i)

            for kv in range(2):
                unit(2 * i + 1, kv, pl.multiple_of(kv * 2048 + c * 512, 512), 512)
            return inner

        lax.fori_loop(EARLY_PAIRS, PAIRS, step, 0)
        heads = []
        for kv in range(2):
            a = acc[:, pl.ds(pl.multiple_of(kv * 2048 + c * 512, 512), 512)]
            if kv == 0:
                o, den = a[0:64], a[64:65]
            else:
                o, den = a[16:80], a[0:1]
            o = o / den
            for pair in range(2):
                two = jnp.concatenate(
                    [
                        o[:, pair * 256 : pair * 256 + 128],
                        o[:, pair * 256 + 128 : pair * 256 + 256],
                    ],
                    axis=0,
                )
                heads.append(jnp.transpose(two).astype(BF16))
        attended = jnp.concatenate(heads, axis=1)
        rows = pl.ds(pl.multiple_of(c * 128, 128), 128)
        for k in (1, 2, 3, 0):
            col = pl.multiple_of(lax.rem(tp + k, n_tp) * 512, 512)
            part = jnp.dot(attended, wov[:, pl.ds(col, 512)], preferred_element_type=F32)
            if k == 0:
                resid[rows, :] = xv[rows, pl.ds(col, 512)].astype(F32) + part
            else:
                rs_send[c, k - 1] = part.astype(BF16)
                reduce_copy(c, k).start()
        return carry

    lax.fori_loop(0, CHUNKS, late, 0)

    def settle(c, carry):
        rows = pl.ds(pl.multiple_of(c * 128, 128), 128)
        total = resid[rows, :]
        for k in range(1, n_tp):
            reduce_copy(c, k).wait_recv()
            total = total + rs_recv[c, k - 1].astype(F32)
        resid[rows, :] = total
        hid_ref[rows, :] = total.astype(BF16)
        square = jnp.sum(total * total, axis=1, keepdims=True)
        ss_send[c] = jnp.transpose(jnp.broadcast_to(square, (128, 128)))[0:8]
        for k in range(1, n_tp):
            square_copy(c, k).start()
        return carry

    lax.fori_loop(0, CHUNKS, settle, 0)

    def finish(c, carry):
        rows = pl.ds(pl.multiple_of(c * 128, 128), 128)
        square = ss_send[c]
        for k in range(1, n_tp):
            square_copy(c, k).wait_recv()
            square = square + ss_recv[c, k - 1]
        column = jnp.transpose(jnp.broadcast_to(square[0:1], (128, 128)))
        scale = lax.rsqrt(column[:, 0:1] * (1.0 / 2048.0) + 1e-05)
        mlp_ref[rows, :] = (resid[rows, :] * scale * ogain_ref[...]).astype(BF16)
        for k in range(1, n_tp):
            reduce_copy(c, k).wait_send()
            square_copy(c, k).wait_send()
        return carry

    lax.fori_loop(0, CHUNKS, finish, 0)

    for copy in [copy_z, copy_y0, copy_y1, copy_c0, copy_c1]:
        copy.wait_send()
    for copy in copies_x0 + copies_x1 + copies_f0 + copies_f1:
        copy.wait_send()

    def cache_wait(k, carry):
        cache_copy(k).wait_send()
        cache_copy(k).wait_recv()
        return carry

    lax.fori_loop(1, n_seq, cache_wait, 0)
    cp_own.wait()


def per_device(
    n_seq,
    n_tp,
    tokens,
    norm_gain,
    query_key_value_weight,
    output_weight,
    out_gain,
    seg_ids,
    earlier_cache,
    decode_owner,
):
    tok, width = tokens.shape
    blocks = earlier_cache.shape[0]
    w = query_key_value_weight.reshape(width, -1)
    wo = output_weight.reshape(-1, width)
    owner = decode_owner[:, 0]
    index = jnp.arange(blocks, dtype=jnp.int32)
    same = (owner[:, None] == owner[None, :]) & (index[:, None] < index[None, :])
    slot = owner * 2 + jnp.sum(same.astype(jnp.int32), axis=0)
    hit = slot[None, :] == jnp.arange(2 * n_seq, dtype=jnp.int32)[:, None]
    inverse = jnp.min(jnp.where(hit, index[None, :], blocks), axis=1)
    rope = jnp.asarray(rope_tables(tok, n_seq))
    share = width // n_tp
    vmem = pl.BlockSpec(memory_space=pltpu.VMEM)
    hbm = pl.BlockSpec(memory_space=pl.ANY)
    smem = pl.BlockSpec(memory_space=pltpu.SMEM)
    dma = pltpu.SemaphoreType.DMA
    hidden, mlp, dec = pl.pallas_call(
        functools.partial(body, n_seq, n_tp),
        out_shape=(
            jax.ShapeDtypeStruct((tok, share), BF16),
            jax.ShapeDtypeStruct((tok, share), BF16),
            jax.ShapeDtypeStruct((2 * n_seq, 2, 2048), BF16),
        ),
        in_specs=[hbm, vmem, hbm, hbm, vmem, vmem, hbm, smem, vmem],
        out_specs=(vmem, vmem, hbm),
        scratch_shapes=[
            pltpu.VMEM((tok, width), BF16),
            pltpu.VMEM((width, 768), BF16),
            pltpu.VMEM((512, width), BF16),
            pltpu.VMEM((blocks + 1, 2, 2048), BF16),
            pltpu.VMEM((2 * n_seq, 2, 2048), BF16),
            pltpu.VMEM((18, PACKET_ROWS, 128), BF16),
            pltpu.VMEM((18, 512, 128), BF16),
            pltpu.VMEM((256, 4096), BF16),
            pltpu.VMEM((8, 4096), F32),
            pltpu.VMEM((80, 4096), F32),
            pltpu.VMEM((tok, share), F32),
            pltpu.VMEM((CHUNKS, 3, 128, share), BF16),
            pltpu.VMEM((CHUNKS, 3, 128, share), BF16),
            pltpu.VMEM((CHUNKS, 8, 128), F32),
            pltpu.VMEM((CHUNKS, 3, 8, 128), F32),
            dma((5,)),
            dma((64,)),
            dma((64,)),
            dma((17,)),
            dma((18,)),
            dma((CHUNKS, 3)),
            dma((CHUNKS, 3)),
            dma((CHUNKS, 3)),
            dma((CHUNKS, 3)),
        ],
        compiler_params=pltpu.CompilerParams(
            collective_id=0, has_side_effects=True, vmem_limit_bytes=58 << 20
        ),
        name="attention_block",
    )(
        tokens,
        norm_gain.reshape(1, -1),
        w,
        wo,
        out_gain.reshape(1, -1),
        seg_ids.reshape(1, -1),
        earlier_cache,
        inverse,
        rope,
    )
    return (hidden, mlp, dec)


def solution(mesh):
    n_seq, n_tp = mesh.shape["seq"], mesh.shape["tp"]
    in_specs = (
        P("seq", None),
        P(),
        P(None, "tp", None),
        P("tp", None, None),
        P("tp"),
        P("seq"),
        P("seq", "tp", None),
        P("seq", None),
    )
    out_specs = (P("seq", "tp"), P("seq", "tp"), P("seq", "tp", None))
    return jax.shard_map(
        functools.partial(per_device, n_seq, n_tp),
        mesh=mesh,
        in_specs=in_specs,
        out_specs=out_specs,
        check_vma=False,
    )
```

```python
import functools
import math

import jax
import jax.numpy as jnp
import numpy as np
from jax import lax
from jax.experimental import pallas as pl
from jax.experimental.pallas import tpu as pltpu
from jax.sharding import PartitionSpec as P

HEAD_SIZE = 64
QUERY_PER_KEY = 4
REQS = 16
BIG = float(2.0**100)
CHUNKS = 4
PACKET_ROWS = 256 + 4 * 80
PAIRS = 8
EARLY_PAIRS = (5, 2)
CACHE_AHEAD = 0
CACHE_STEP = 8
MESH = pl.DeviceIdType.MESH
F32 = jnp.float32
BF16 = jnp.bfloat16


def rope_tables(tok, blocks):
    half = HEAD_SIZE // 2
    freq = 500000.0 ** (-2.0 * np.arange(half) / HEAD_SIZE)
    inner = freq[:, None] * np.arange(tok)[None, :]
    outer = freq[:, None] * (np.arange(128) * tok)[None, :]
    parts = [np.cos(inner), np.sin(inner), np.cos(outer), np.sin(outer)]
    return np.concatenate(parts, axis=1).astype(np.float32)


def body(
    n_seq,
    n_tp,
    x_hbm,
    gain_ref,
    w_hbm,
    wo_hbm,
    ogain_ref,
    seg_ref,
    cache_hbm,
    inv_ref,
    rope_ref,
    hid_ref,
    mlp_ref,
    dec_hbm,
    xv,
    wv,
    wov,
    cachev,
    outg,
    kvb,
    kf,
    qt,
    mx,
    acc,
    resid,
    att,
    att_in,
    wg,
    ss_send,
    ss_recv,
    lsem,
    c_ssem,
    c_rsem,
    kv_ssem,
    kv_rsem,
    r_ssem,
    r_rsem,
    s_ssem,
    s_rsem,
    w_ssem,
    w_rsem,
):
    me = lax.axis_index("seq")
    tp = lax.axis_index("tp")
    core = lax.rem(me, 2)
    zh = lax.rem(me // 2, 2)
    xx = lax.rem(me // 4, 4)
    yy = me // 16
    slab = (me // 16) * 16
    tok = 512

    cp_cache = pltpu.make_async_copy(cache_hbm, cachev.at[pl.ds(0, 64)], lsem.at[0])
    cp_x = pltpu.make_async_copy(x_hbm, xv, lsem.at[1])
    cp_w = pltpu.make_async_copy(w_hbm, wv, lsem.at[2])
    cp_wo = pltpu.make_async_copy(wo_hbm, wov, lsem.at[3])
    cp_cache.start()
    cp_x.start()
    cp_w.start()
    cp_wo.start()

    barrier = pltpu.get_barrier_semaphore()

    def greet(k, carry):
        pl.semaphore_signal(
            barrier,
            inc=1,
            device_id={"seq": lax.rem(me + k, n_seq), "tp": tp},
            device_id_type=MESH,
        )
        return carry

    lax.fori_loop(1, n_seq, greet, 0)
    for k in range(1, n_tp):
        pl.semaphore_signal(
            barrier,
            inc=1,
            device_id={"seq": me, "tp": lax.rem(tp + k, n_tp)},
            device_id_type=MESH,
        )

    cachev[64] = jnp.zeros((2, 2048), BF16)
    cp_cache.wait()

    def place(r, carry):
        outg[r] = cachev[inv_ref[r]]
        return carry

    lax.fori_loop(0, 2 * n_seq, place, 0)
    pl.semaphore_wait(barrier, n_seq - 1 + n_tp - 1)

    def cache_copy(k):
        to_y = lax.rem(yy + lax.rem(k, 32) // 8, 4)
        to_x = lax.rem(xx + lax.rem(k, 8) // 2, 4)
        to_z = lax.rem(zh + k // 32, 2)
        to_c = lax.rem(core + lax.rem(k, 2), 2)
        to = ((to_y * 4 + to_x) * 2 + to_z) * 2 + to_c
        return pltpu.make_async_remote_copy(
            src_ref=outg.at[pl.ds(2 * to, 2)],
            dst_ref=dec_hbm.at[pl.ds(2 * me, 2)],
            send_sem=c_ssem.at[k],
            recv_sem=c_rsem.at[k],
            device_id={"seq": to, "tp": tp},
            device_id_type=MESH,
        )

    def cache_start(k, carry):
        cache_copy(k).start()
        return carry

    cp_own = pltpu.make_async_copy(
        outg.at[pl.ds(2 * me, 2)], dec_hbm.at[pl.ds(2 * me, 2)], lsem.at[4]
    )
    cp_own.start()

    share_at = core * 16 + yy * 4 + xx

    def weight_z(k):
        to = lax.rem(tp + k, n_tp)
        return pltpu.make_async_remote_copy(
            src_ref=wov.at[
                pl.ds(pl.multiple_of(share_at * 16, 16), 16),
                pl.ds(pl.multiple_of(to * 512, 512), 512),
            ],
            dst_ref=wg.at[share_at, k - 1],
            send_sem=w_ssem.at[k - 1],
            recv_sem=w_rsem.at[k - 1],
            device_id={"seq": me, "tp": to},
            device_id_type=MESH,
        )

    def weight_part(at, count, sem, to):
        return pltpu.make_async_remote_copy(
            src_ref=wg.at[pl.ds(at, count)],
            dst_ref=wg.at[pl.ds(at, count)],
            send_sem=w_ssem.at[sem],
            recv_sem=w_rsem.at[sem],
            device_id={"seq": to, "tp": tp},
            device_id_type=MESH,
        )

    weights_z = [weight_z(k) for k in (1, 2, 3)]
    weights_x = [
        weight_part(share_at, 1, 2 + j, slab + lax.rem(me - slab + 4 * j, 16)) for j in (1, 2, 3)
    ]
    weights_y = [
        weight_part(core * 16 + yy * 4, 4, 5 + j, lax.rem(me + 16 * j, n_seq)) for j in (1, 2, 3)
    ]
    weight_c = weight_part(core * 16, 16, 9, me + 1 - 2 * core)
    cp_wo.wait()
    for copy in weights_z:
        copy.start()
    lax.fori_loop(1, 32, cache_start, 0)

    lane = lax.broadcasted_iota(jnp.int32, (32, 128), 1)
    here = lane == me
    cos_b = jnp.sum(jnp.where(here, rope_ref[:, 2 * tok : 2 * tok + 128], 0.0), axis=1, keepdims=True)
    sin_b = jnp.sum(
        jnp.where(here, rope_ref[:, 2 * tok + 128 : 2 * tok + 256], 0.0), axis=1, keepdims=True
    )
    q_scale = HEAD_SIZE ** (-0.5) * math.log2(math.e)

    seg = seg_ref[...].astype(F32)
    seg0 = jnp.min(seg, axis=1, keepdims=True)
    carried_in = seg == seg0
    first = jnp.zeros((1, tok), F32)
    for r in range(1, REQS):
        below = jnp.sum(jnp.where(seg < r, 1.0, 0.0), axis=1, keepdims=True)
        first = jnp.where(seg == r, below, first)
    a_bias = jnp.where(carried_in, 0.0, -BIG)

    row16 = lax.broadcasted_iota(jnp.int32, (16, 512), 0)
    for c in range(CHUNKS):
        ab = a_bias[:, c * 128 : (c + 1) * 128]
        ab4 = jnp.concatenate([ab, ab, ab, ab], axis=1)
        feat = jnp.where(row16 == 0, ab4, jnp.where(row16 == 1, 1.0, 0.0)).astype(BF16)
        for kv in range(2):
            lanes = slice(kv * 2048 + c * 512, kv * 2048 + c * 512 + 512)
            for half in range(2):
                qt[half, 128:144, lanes] = feat
                qt[half, 144:256, lanes] = jnp.zeros((112, 512), BF16)
                qt[half, (1 - half) * 64 : (1 - half) * 64 + 64, lanes] = jnp.zeros((64, 512), BF16)

    cp_x.wait()
    cp_w.wait()
    gain = gain_ref[...]
    aux_row = lax.broadcasted_iota(jnp.int32, (16, 128), 0)
    keys_t = [[None] * CHUNKS, [None] * CHUNKS]
    for c in range(CHUNKS):
        cols = slice(c * 128, (c + 1) * 128)
        xc = xv[cols, :].astype(F32)
        ms = jnp.mean(xc * xc, axis=1, keepdims=True)
        normed = (xc * lax.rsqrt(ms + 1e-05) * gain).astype(BF16)
        proj = jnp.dot(normed, wv[...], preferred_element_type=F32)
        ci = rope_ref[:, c * 128 : (c + 1) * 128]
        si = rope_ref[:, tok + c * 128 : tok + (c + 1) * 128]
        cos = ci * cos_b - si * sin_b
        sin = si * cos_b + ci * sin_b
        cos_q, sin_q = cos * q_scale, sin * q_scale

        def rot(a, co, sn):
            a1, a2 = a[0:32], a[32:64]
            return jnp.concatenate([a1 * co - a2 * sn, a2 * co + a1 * sn], axis=0)

        for kv in range(2):
            for pair in range(2):
                at = kv * 384 + pair * 128
                tr = jnp.transpose(proj[:, at : at + 128])
                for g2 in range(2):
                    g = pair * 2 + g2
                    lane0 = kv * 2048 + c * 512 + g * 128
                    q = rot(tr[g2 * 64 : g2 * 64 + 64], cos_q, sin_q).astype(BF16)
                    qt[0, 0:64, lane0 : lane0 + 128] = q
                    qt[1, 64:128, lane0 : lane0 + 128] = q
            tr = jnp.transpose(proj[:, kv * 384 + 256 : kv * 384 + 384])
            keys_t[kv][c] = rot(tr[0:64], cos, sin)
            base = 256 + c * 80
            kvb[kv * 18, base : base + 64, :] = tr[64:128].astype(BF16)
            kvb[kv * 18, base + 64 : base + 80, :] = jnp.where(
                aux_row == 0, 1.0, jnp.where(aux_row == 1, seg[:, cols], 0.0)
            ).astype(BF16)
    for kv in range(2):
        for j in range(2):
            kvb[kv * 18, j * 128 : (j + 1) * 128, :] = jnp.transpose(
                jnp.concatenate([keys_t[kv][j], keys_t[kv][j + 2]], axis=0)
            ).astype(BF16)

    def packet(h, src, dst, sem, seq_to):
        return pltpu.make_async_remote_copy(
            src_ref=kvb.at[18 * h + src],
            dst_ref=kvb.at[18 * h + dst],
            send_sem=kv_ssem.at[17 * h + sem],
            recv_sem=kv_rsem.at[18 * h + dst],
            device_id={"seq": seq_to, "tp": tp},
            device_id_type=MESH,
        )

    a1 = jnp.where(zh == 1, 9, 17)
    b1 = jnp.where(zh == 1, 17, 9)
    z_to = me + 2 - 4 * zh
    y_to = lax.rem(me + 16, n_seq)
    sib = me + 1 - 2 * core

    def x_to(j):
        return slab + lax.rem(me - slab + 16 - 4 * j, 16)

    def x_src(j, a, b):
        dest_x = lax.rem(xx + 4 - j, 4)
        return jnp.where(dest_x > xx, a, b)

    def copy_z(h):
        return packet(h, 0, jnp.where(zh == 0, 9, 17), 0, z_to)

    def copy_y0(h):
        return packet(h, 0, 1, 1, y_to)

    def copy_y1(h):
        return packet(h, a1, b1, 2, y_to)

    def copies_x0(h):
        return [packet(h, x_src(j, 0, 1), 2 + j, 2 + j, x_to(j)) for j in (1, 2, 3)]

    def copies_x1(h):
        return [packet(h, x_src(j, a1, b1), 10 + j, 5 + j, x_to(j)) for j in (1, 2, 3)]

    def copy_c0(h):
        return packet(h, jnp.where(core == 0, 0, 1), 2, 9, sib)

    def copy_c1(h):
        return packet(h, 9, 10, 10, sib)

    def copies_f0(h):
        return [packet(h, 2 + j, 5 + j, 10 + j, sib) for j in (1, 2, 3)]

    def copies_f1(h):
        return [packet(h, 10 + j, 13 + j, 13 + j, sib) for j in (1, 2, 3)]

    def arrived(h, slot):
        here_at = kvb.at[18 * h + slot]
        pltpu.make_async_copy(here_at, here_at, kv_rsem.at[18 * h + slot]).wait()

    for h in range(2):
        copy_y0(h).start()
        copy_z(h).start()
    for copy in weights_z:
        copy.wait_recv()
    for copy in weights_x:
        copy.start()

    def values_of(h, slot, half):
        at = 256 + half * 160
        return jnp.concatenate(
            [kvb[18 * h + slot, at : at + 80, :], kvb[18 * h + slot, at + 80 : at + 160, :]], axis=1
        )

    for c in range(CHUNKS):
        span = (c + 1) * 128
        key_at = lax.broadcasted_iota(jnp.int32, (span, 128), 0).astype(F32)
        query_at = lax.broadcasted_iota(jnp.int32, (span, 128), 1).astype(F32) + c * 128
        allowed1 = (key_at <= query_at) & (key_at >= first[:, c * 128 : (c + 1) * 128])
        bias1 = jnp.where(allowed1, 0.0, -BIG)
        bias = jnp.concatenate([bias1, bias1, bias1, bias1], axis=1)
        for kv in range(2):
            lanes = slice(kv * 2048 + c * 512, kv * 2048 + c * 512 + 512)
            parts = [
                jnp.dot(
                    kvb[18 * kv, 0 : min(span, 256), :],
                    qt[0, 0:128, lanes],
                    preferred_element_type=F32,
                )
            ]
            vals = [values_of(kv, 0, 0)]
            if span > 256:
                parts.append(
                    jnp.dot(
                        kvb[18 * kv, 0 : span - 256, :],
                        qt[1, 0:128, lanes],
                        preferred_element_type=F32,
                    )
                )
                vals.append(values_of(kv, 0, 1))
            s = jnp.concatenate(parts, axis=0) + bias
            top = jnp.max(s, axis=0, keepdims=True)
            p = jnp.exp2(s - top).astype(BF16)
            mx[:, lanes] = jnp.broadcast_to(top, (8, 512))
            acc[:, lanes] = jnp.dot(
                jnp.concatenate(vals, axis=1)[:, 0:span], p, preferred_element_type=F32
            )

    u_at = lax.broadcasted_iota(jnp.int32, (512, 128), 0).astype(F32)
    f_lane = lax.broadcasted_iota(jnp.int32, (512, 128), 1)

    def prepare(slot):
        strange = jnp.zeros((1, 128), F32)
        for j in range(4):
            aux = kvb[slot, 256 + j * 80 + 64 : 256 + j * 80 + 80, :].astype(F32)
            strange = strange + jnp.where(aux[1:2, :] != seg0, 1.0, 0.0)
        count = jnp.sum(strange, axis=1, keepdims=True)
        bias = jnp.where(u_at < count, -BIG, 0.0)
        kf[slot] = jnp.where(f_lane == 0, 1.0, jnp.where(f_lane == 1, bias, 0.0)).astype(BF16)

    def unit(slot, h, start, width):
        lanes = pl.ds(start, width)
        scores, vals = [], []
        for half in range(2):
            k = jnp.concatenate(
                [
                    jnp.concatenate(
                        [kvb[18 * h + s, 0:256, :], kf[s, half * 256 : half * 256 + 256, :]], axis=1
                    )
                    for s in (slot, slot + 1)
                ],
                axis=0,
            )
            scores.append(jnp.dot(k, qt[half, :, lanes], preferred_element_type=F32))
            vals.append(
                jnp.concatenate([values_of(h, slot, half), values_of(h, slot + 1, half)], axis=1)
            )
        old = mx[:, lanes]
        tops = [jnp.max(s, axis=0, keepdims=True) for s in scores]
        new = jnp.maximum(old, jnp.maximum(tops[0], tops[1]))
        factor = jnp.exp2(old - new)
        total = acc[:, lanes] * factor[0:1]
        for s, v in zip(scores, vals):
            p = jnp.exp2(s - new[0:1]).astype(BF16)
            total = total + jnp.dot(v, p, preferred_element_type=F32)
        acc[:, lanes] = total
        mx[:, lanes] = new

    def spread(h):
        arrived(h, 1)
        for copy in copies_x0(h):
            copy.start()
        copy_c0(h).start()

    def spread_y(h):
        arrived(h, a1)
        copy_y1(h).start()

    def spread_late(h):
        arrived(h, b1)
        for copy in copies_x1(h):
            copy.start()
        copy_c1(h).start()

    def attended_copy(piece, k):
        return pltpu.make_async_remote_copy(
            src_ref=att.at[piece],
            dst_ref=att_in.at[piece, k - 1],
            send_sem=r_ssem.at[piece, k - 1],
            recv_sem=r_rsem.at[piece, k - 1],
            device_id={"seq": me, "tp": lax.rem(tp + k, n_tp)},
            device_id_type=MESH,
        )

    def conclude(h, c):
        a = acc[:, pl.ds(pl.multiple_of(h * 2048 + c * 512, 512), 512)]
        o = a[0:64] / a[64:65]
        for pair in range(2):
            two = jnp.concatenate(
                [o[:, pair * 256 : pair * 256 + 128], o[:, pair * 256 + 128 : pair * 256 + 256]],
                axis=0,
            )
            att[h * 4 + c, :, pair * 128 : pair * 128 + 128] = jnp.transpose(two).astype(BF16)
        for k in (2, 3, 1):
            attended_copy(h * 4 + c, k).start()

    def arrive0(i):
        @pl.when(i == 0)
        def _():
            spread(0)

        @pl.when(i == 1)
        def _():
            spread(1)
            spread_y(0)

        @pl.when(i == 2)
        def _():
            spread_late(0)
            for copy in weights_x:
                copy.wait_recv()
            for copy in weights_y:
                copy.start()

        @pl.when(i == 3)
        def _():
            spread_y(1)

        @pl.when(i == 4)
        def _():
            for slot in (3, 4, 5):
                arrived(1, slot)
            for copy in copies_f0(1):
                copy.start()

        @pl.when(i == 5)
        def _():
            spread_late(1)

        for j in range(2):
            slot = 2 * i + 1 + j

            @pl.when((slot != 1) & (slot != 9))
            def _():
                arrived(0, slot)

            @pl.when(((slot >= 3) & (slot <= 5)) | ((slot >= 11) & (slot <= 13)))
            def _():
                wave = jnp.where(slot >= 11, 1, 0)
                packet(0, slot, slot + 3, slot + 8 - 5 * wave, sib).start()

            prepare(slot)

        @pl.when((i >= 3) & (i <= 6))
        def _():
            at = 32 + CACHE_AHEAD + (i - 3) * CACHE_STEP
            lax.fori_loop(at, at + CACHE_STEP, cache_start, 0)

    def early0(i, carry):
        arrive0(i)
        unit(2 * i + 1, 0, 0, 2048)
        return carry

    lax.fori_loop(0, EARLY_PAIRS[0], early0, 0)

    def late0(c, carry):
        def step(i, inner):
            @pl.when(c == 0)
            def _():
                arrive0(i)

            unit(2 * i + 1, 0, pl.multiple_of(c * 512, 512), 512)
            return inner

        lax.fori_loop(EARLY_PAIRS[0], PAIRS, step, 0)
        conclude(0, c)
        return carry

    lax.fori_loop(0, CHUNKS, late0, 0)

    def arrive1(i):
        @pl.when(i == 0)
        def _():
            for copy in weights_y:
                copy.wait_recv()
            weight_c.start()

        @pl.when(i == 1)
        def _():
            for slot in (11, 12, 13):
                arrived(1, slot)
            for copy in copies_f1(1):
                copy.start()

        for j in range(2):
            slot = 2 * i + 1 + j

            @pl.when(
                (slot == 2)
                | (slot == 10)
                | ((slot >= 6) & (slot <= 8))
                | ((slot >= 14) & (slot <= 16))
            )
            def _():
                arrived(1, slot)

    def early1(i, carry):
        arrive1(i)
        unit(2 * i + 1, 1, 2048, 2048)
        return carry

    lax.fori_loop(0, EARLY_PAIRS[1], early1, 0)

    def square_copy(c, k):
        return pltpu.make_async_remote_copy(
            src_ref=ss_send.at[c],
            dst_ref=ss_recv.at[c, k - 1],
            send_sem=s_ssem.at[c, k - 1],
            recv_sem=s_rsem.at[c, k - 1],
            device_id={"seq": me, "tp": lax.rem(tp + k, n_tp)},
            device_id_type=MESH,
        )

    own_col = pl.ds(pl.multiple_of(tp * 512, 512), 512)

    def weight_of(k, h):
        if k == 0:
            return wov[h * 256 : h * 256 + 256, own_col]
        return jnp.concatenate([wg[h * 16 + e, k - 1] for e in range(16)], axis=0)

    def first_half():
        for k in range(1, n_tp):
            for c in range(CHUNKS):
                attended_copy(c, k).wait_recv()
        weight_c.wait_recv()
        total = xv[:, own_col].astype(F32)
        for k in range(n_tp):
            a = jnp.concatenate(
                [att[c] if k == 0 else att_in[c, k - 1] for c in range(CHUNKS)], axis=0
            )
            total = total + jnp.dot(a, weight_of(k, 0), preferred_element_type=F32)
        resid[...] = total

    def settle(c):
        rows = pl.ds(pl.multiple_of(c * 128, 128), 128)
        total = resid[rows, :]
        for k in range(n_tp):
            if k > 0:
                attended_copy(4 + c, k).wait_recv()
            a = att[4 + c] if k == 0 else att_in[4 + c, k - 1]
            total = total + jnp.dot(a, weight_of(k, 1), preferred_element_type=F32)
        resid[rows, :] = total
        hid_ref[rows, :] = total.astype(BF16)
        square = jnp.sum(total * total, axis=1, keepdims=True)
        ss_send[c] = jnp.transpose(jnp.broadcast_to(square, (128, 128)))[0:8]
        for k in range(1, n_tp):
            square_copy(c, k).start()

    def late(c, carry):
        def step(i, inner):
            @pl.when(c == 0)
            def _():
                arrive1(i)

            unit(2 * i + 1, 1, pl.multiple_of(2048 + c * 512, 512), 512)
            return inner

        lax.fori_loop(EARLY_PAIRS[1], PAIRS, step, 0)
        conclude(1, c)

        @pl.when(c == 1)
        def _():
            first_half()

        @pl.when(c > 0)
        def _():
            settle(c - 1)

        return carry

    lax.fori_loop(0, CHUNKS, late, 0)
    settle(CHUNKS - 1)

    def finish(c, carry):
        rows = pl.ds(pl.multiple_of(c * 128, 128), 128)
        square = ss_send[c]
        for k in range(1, n_tp):
            square_copy(c, k).wait_recv()
            square = square + ss_recv[c, k - 1]
        column = jnp.transpose(jnp.broadcast_to(square[0:1], (128, 128)))
        scale = lax.rsqrt(column[:, 0:1] * (1.0 / 2048.0) + 1e-05)
        mlp_ref[rows, :] = (resid[rows, :] * scale * ogain_ref[...]).astype(BF16)
        for k in range(1, n_tp):
            attended_copy(c, k).wait_send()
            attended_copy(4 + c, k).wait_send()
            square_copy(c, k).wait_send()
        return carry

    lax.fori_loop(0, CHUNKS, finish, 0)

    for h in range(2):
        for copy in [copy_z(h), copy_y0(h), copy_y1(h), copy_c0(h), copy_c1(h)]:
            copy.wait_send()
        for copy in copies_x0(h) + copies_x1(h) + copies_f0(h) + copies_f1(h):
            copy.wait_send()
    for copy in weights_z + weights_x + weights_y + [weight_c]:
        copy.wait_send()

    def cache_wait(k, carry):
        cache_copy(k).wait_send()
        cache_copy(k).wait_recv()
        return carry

    lax.fori_loop(1, n_seq, cache_wait, 0)
    cp_own.wait()


def hand_over(hid, mlp, dec, hid_out, mlp_out, dec_out, sems):
    pieces = [(hid, hid_out, 0), (mlp, mlp_out, 1)]
    copies = [pltpu.make_async_copy(a, b, sems.at[k]) for a, b, k in pieces]
    for k in range(4):
        rows = pl.ds(32 * k, 32)
        copies.append(pltpu.make_async_copy(dec.at[rows], dec_out.at[rows], sems.at[2 + k]))
    for copy in copies:
        copy.start()
    for copy in copies:
        copy.wait()


def per_device(
    n_seq,
    n_tp,
    tokens,
    norm_gain,
    query_key_value_weight,
    output_weight,
    out_gain,
    seg_ids,
    earlier_cache,
    decode_owner,
):
    tok, width = tokens.shape
    blocks = earlier_cache.shape[0]
    w = query_key_value_weight.reshape(width, -1)
    wo = output_weight.reshape(-1, width)
    owner = decode_owner[:, 0]
    index = jnp.arange(blocks, dtype=jnp.int32)
    same = (owner[:, None] == owner[None, :]) & (index[:, None] < index[None, :])
    slot = owner * 2 + jnp.sum(same.astype(jnp.int32), axis=0)
    hit = slot[None, :] == jnp.arange(2 * n_seq, dtype=jnp.int32)[:, None]
    inverse = jnp.min(jnp.where(hit, index[None, :], blocks), axis=1)
    rope = jnp.asarray(rope_tables(tok, n_seq))
    share = width // n_tp
    vmem = pl.BlockSpec(memory_space=pltpu.VMEM)
    hbm = pl.BlockSpec(memory_space=pl.ANY)
    smem = pl.BlockSpec(memory_space=pltpu.SMEM)
    dma = pltpu.SemaphoreType.DMA
    hidden, mlp, dec = pl.pallas_call(
        functools.partial(body, n_seq, n_tp),
        out_shape=(
            jax.ShapeDtypeStruct((tok, share), BF16),
            jax.ShapeDtypeStruct((tok, share), BF16),
            jax.ShapeDtypeStruct((2 * n_seq, 2, 2048), BF16),
        ),
        in_specs=[hbm, vmem, hbm, hbm, vmem, vmem, hbm, smem, vmem],
        out_specs=(vmem, vmem, hbm),
        scratch_shapes=[
            pltpu.VMEM((tok, width), BF16),
            pltpu.VMEM((width, 768), BF16),
            pltpu.VMEM((512, width), BF16),
            pltpu.VMEM((blocks + 1, 2, 2048), BF16),
            pltpu.VMEM((2 * n_seq, 2, 2048), BF16),
            pltpu.VMEM((36, PACKET_ROWS, 128), BF16),
            pltpu.VMEM((18, 512, 128), BF16),
            pltpu.VMEM((2, 256, 4096), BF16),
            pltpu.VMEM((8, 4096), F32),
            pltpu.VMEM((80, 4096), F32),
            pltpu.VMEM((tok, share), F32),
            pltpu.VMEM((2 * CHUNKS, 128, 256), BF16),
            pltpu.VMEM((2 * CHUNKS, 3, 128, 256), BF16),
            pltpu.VMEM((32, 3, 16, share), BF16),
            pltpu.VMEM((CHUNKS, 8, 128), F32),
            pltpu.VMEM((CHUNKS, 3, 8, 128), F32),
            dma((5,)),
            dma((64,)),
            dma((64,)),
            dma((34,)),
            dma((36,)),
            dma((2 * CHUNKS, 3)),
            dma((2 * CHUNKS, 3)),
            dma((CHUNKS, 3)),
            dma((CHUNKS, 3)),
            dma((10,)),
            dma((10,)),
        ],
        compiler_params=pltpu.CompilerParams(
            collective_id=0, has_side_effects=True, vmem_limit_bytes=58 << 20
        ),
        name="attention_block",
    )(
        tokens,
        norm_gain.reshape(1, -1),
        w,
        wo,
        out_gain.reshape(1, -1),
        seg_ids.reshape(1, -1),
        earlier_cache,
        inverse,
        rope,
    )
    return pl.pallas_call(
        hand_over,
        out_shape=(
            jax.ShapeDtypeStruct((tok, share), BF16),
            jax.ShapeDtypeStruct((tok, share), BF16),
            jax.ShapeDtypeStruct((2 * n_seq, 2, 2048), BF16),
        ),
        in_specs=[hbm, hbm, hbm],
        out_specs=(hbm, hbm, hbm),
        scratch_shapes=[dma((6,))],
        name="hand_over",
    )(hidden, mlp, dec)


def solution(mesh):
    n_seq, n_tp = mesh.shape["seq"], mesh.shape["tp"]
    in_specs = (
        P("seq", None),
        P(),
        P(None, "tp", None),
        P("tp", None, None),
        P("tp"),
        P("seq"),
        P("seq", "tp", None),
        P("seq", None),
    )
    out_specs = (P("seq", "tp"), P("seq", "tp"), P("seq", "tp", None))
    return jax.shard_map(
        functools.partial(per_device, n_seq, n_tp),
        mesh=mesh,
        in_specs=in_specs,
        out_specs=out_specs,
        check_vma=False,
    )
```

```python
import functools
import math

import jax
import jax.numpy as jnp
import numpy as np
from jax import lax
from jax.experimental import pallas as pl
from jax.experimental.pallas import tpu as pltpu
from jax.sharding import PartitionSpec as P

HEAD_SIZE = 64
QUERY_PER_KEY = 4
REQS = 16
BIG = float(2.0**100)
CHUNKS = 4
PACKET_ROWS = 256 + 4 * 80
PAIRS = 8
EARLY_PAIRS = (5, 2)
CACHE_AHEAD = 0
CACHE_STEP = 8
MESH = pl.DeviceIdType.MESH
F32 = jnp.float32
BF16 = jnp.bfloat16


def rope_tables(tok, blocks):
    half = HEAD_SIZE // 2
    freq = 500000.0 ** (-2.0 * np.arange(half) / HEAD_SIZE)
    inner = freq[:, None] * np.arange(tok)[None, :]
    outer = freq[:, None] * (np.arange(128) * tok)[None, :]
    parts = [np.cos(inner), np.sin(inner), np.cos(outer), np.sin(outer)]
    return np.concatenate(parts, axis=1).astype(np.float32)


def body(
    n_seq,
    n_tp,
    x_hbm,
    gain_ref,
    w_hbm,
    wo_hbm,
    ogain_ref,
    seg_ref,
    cache_hbm,
    inv_ref,
    rope_ref,
    hid_ref,
    mlp_ref,
    dec_hbm,
    xv,
    wv,
    wov,
    cachev,
    outg,
    kvb,
    kf,
    qt,
    mx,
    acc,
    resid,
    att,
    att_in,
    wg,
    ss_send,
    ss_recv,
    lsem,
    c_ssem,
    c_rsem,
    kv_ssem,
    kv_rsem,
    r_ssem,
    r_rsem,
    s_ssem,
    s_rsem,
    w_ssem,
    w_rsem,
):
    me = lax.axis_index("seq")
    tp = lax.axis_index("tp")
    core = lax.rem(me, 2)
    zh = lax.rem(me // 2, 2)
    xx = lax.rem(me // 4, 4)
    yy = me // 16
    slab = (me // 16) * 16
    tok = 512

    cp_cache = pltpu.make_async_copy(cache_hbm, cachev.at[pl.ds(0, 64)], lsem.at[0])
    cp_x = pltpu.make_async_copy(x_hbm, xv, lsem.at[1])
    cp_w = pltpu.make_async_copy(w_hbm, wv, lsem.at[2])
    cp_wo = pltpu.make_async_copy(wo_hbm, wov, lsem.at[3])
    cp_cache.start()
    cp_x.start()
    cp_w.start()
    cp_wo.start()

    barrier = pltpu.get_barrier_semaphore()

    def greet(k, carry):
        pl.semaphore_signal(
            barrier,
            inc=1,
            device_id={"seq": lax.rem(me + k, n_seq), "tp": tp},
            device_id_type=MESH,
        )
        return carry

    lax.fori_loop(1, n_seq, greet, 0)
    for k in range(1, n_tp):
        pl.semaphore_signal(
            barrier,
            inc=1,
            device_id={"seq": me, "tp": lax.rem(tp + k, n_tp)},
            device_id_type=MESH,
        )

    cachev[64] = jnp.zeros((2, 2048), BF16)
    cp_cache.wait()

    def place(r, carry):
        outg[r] = cachev[inv_ref[r]]
        return carry

    lax.fori_loop(0, 2 * n_seq, place, 0)
    pl.semaphore_wait(barrier, n_seq - 1 + n_tp - 1)

    def cache_copy(k):
        to_y = lax.rem(yy + lax.rem(k, 32) // 8, 4)
        to_x = lax.rem(xx + lax.rem(k, 8) // 2, 4)
        to_z = lax.rem(zh + k // 32, 2)
        to_c = lax.rem(core + lax.rem(k, 2), 2)
        to = ((to_y * 4 + to_x) * 2 + to_z) * 2 + to_c
        return pltpu.make_async_remote_copy(
            src_ref=outg.at[pl.ds(2 * to, 2)],
            dst_ref=dec_hbm.at[pl.ds(2 * me, 2)],
            send_sem=c_ssem.at[k],
            recv_sem=c_rsem.at[k],
            device_id={"seq": to, "tp": tp},
            device_id_type=MESH,
        )

    def cache_start(k, carry):
        cache_copy(k).start()
        return carry

    cp_own = pltpu.make_async_copy(
        outg.at[pl.ds(2 * me, 2)], dec_hbm.at[pl.ds(2 * me, 2)], lsem.at[4]
    )
    cp_own.start()

    share_at = core * 16 + yy * 4 + xx

    def weight_z(k):
        to = lax.rem(tp + k, n_tp)
        return pltpu.make_async_remote_copy(
            src_ref=wov.at[
                pl.ds(pl.multiple_of(share_at * 16, 16), 16),
                pl.ds(pl.multiple_of(to * 512, 512), 512),
            ],
            dst_ref=wg.at[share_at, k - 1],
            send_sem=w_ssem.at[k - 1],
            recv_sem=w_rsem.at[k - 1],
            device_id={"seq": me, "tp": to},
            device_id_type=MESH,
        )

    def weight_part(at, count, sem, to):
        return pltpu.make_async_remote_copy(
            src_ref=wg.at[pl.ds(at, count)],
            dst_ref=wg.at[pl.ds(at, count)],
            send_sem=w_ssem.at[sem],
            recv_sem=w_rsem.at[sem],
            device_id={"seq": to, "tp": tp},
            device_id_type=MESH,
        )

    weights_z = [weight_z(k) for k in (1, 2, 3)]
    weights_x = [
        weight_part(share_at, 1, 2 + j, slab + lax.rem(me - slab + 4 * j, 16)) for j in (1, 2, 3)
    ]
    weights_y = [
        weight_part(core * 16 + yy * 4, 4, 5 + j, lax.rem(me + 16 * j, n_seq)) for j in (1, 2, 3)
    ]
    weight_c = weight_part(core * 16, 16, 9, me + 1 - 2 * core)
    cp_wo.wait()
    for copy in weights_z:
        copy.start()
    lax.fori_loop(1, 32, cache_start, 0)

    lane = lax.broadcasted_iota(jnp.int32, (32, 128), 1)
    here = lane == me
    cos_b = jnp.sum(jnp.where(here, rope_ref[:, 2 * tok : 2 * tok + 128], 0.0), axis=1, keepdims=True)
    sin_b = jnp.sum(
        jnp.where(here, rope_ref[:, 2 * tok + 128 : 2 * tok + 256], 0.0), axis=1, keepdims=True
    )
    q_scale = HEAD_SIZE ** (-0.5) * math.log2(math.e)

    seg = seg_ref[...].astype(F32)
    seg0 = jnp.min(seg, axis=1, keepdims=True)
    carried_in = seg == seg0
    first = jnp.zeros((1, tok), F32)
    for r in range(1, REQS):
        below = jnp.sum(jnp.where(seg < r, 1.0, 0.0), axis=1, keepdims=True)
        first = jnp.where(seg == r, below, first)
    a_bias = jnp.where(carried_in, 0.0, -BIG)

    row16 = lax.broadcasted_iota(jnp.int32, (16, 512), 0)
    for c in range(CHUNKS):
        ab = a_bias[:, c * 128 : (c + 1) * 128]
        ab4 = jnp.concatenate([ab, ab, ab, ab], axis=1)
        feat = jnp.where(row16 == 0, ab4, jnp.where(row16 == 1, 1.0, 0.0)).astype(BF16)
        for kv in range(2):
            lanes = slice(kv * 2048 + c * 512, kv * 2048 + c * 512 + 512)
            for half in range(2):
                qt[half, 128:144, lanes] = feat
                qt[half, 144:256, lanes] = jnp.zeros((112, 512), BF16)
                qt[half, (1 - half) * 64 : (1 - half) * 64 + 64, lanes] = jnp.zeros((64, 512), BF16)

    cp_x.wait()
    cp_w.wait()
    gain = gain_ref[...]
    aux_row = lax.broadcasted_iota(jnp.int32, (16, 128), 0)
    keys_t = [[None] * CHUNKS, [None] * CHUNKS]
    for c in range(CHUNKS):
        cols = slice(c * 128, (c + 1) * 128)
        xc = xv[cols, :].astype(F32)
        ms = jnp.mean(xc * xc, axis=1, keepdims=True)
        normed = (xc * lax.rsqrt(ms + 1e-05) * gain).astype(BF16)
        proj = jnp.dot(normed, wv[...], preferred_element_type=F32)
        ci = rope_ref[:, c * 128 : (c + 1) * 128]
        si = rope_ref[:, tok + c * 128 : tok + (c + 1) * 128]
        cos = ci * cos_b - si * sin_b
        sin = si * cos_b + ci * sin_b
        cos_q, sin_q = cos * q_scale, sin * q_scale

        def rot(a, co, sn):
            a1, a2 = a[0:32], a[32:64]
            return jnp.concatenate([a1 * co - a2 * sn, a2 * co + a1 * sn], axis=0)

        for kv in range(2):
            for pair in range(2):
                at = kv * 384 + pair * 128
                tr = jnp.transpose(proj[:, at : at + 128])
                for g2 in range(2):
                    g = pair * 2 + g2
                    lane0 = kv * 2048 + c * 512 + g * 128
                    q = rot(tr[g2 * 64 : g2 * 64 + 64], cos_q, sin_q).astype(BF16)
                    qt[0, 0:64, lane0 : lane0 + 128] = q
                    qt[1, 64:128, lane0 : lane0 + 128] = q
            tr = jnp.transpose(proj[:, kv * 384 + 256 : kv * 384 + 384])
            keys_t[kv][c] = rot(tr[0:64], cos, sin)
            base = 256 + c * 80
            kvb[kv * 18, base : base + 64, :] = tr[64:128].astype(BF16)
            kvb[kv * 18, base + 64 : base + 80, :] = jnp.where(
                aux_row == 0, 1.0, jnp.where(aux_row == 1, seg[:, cols], 0.0)
            ).astype(BF16)
    for kv in range(2):
        for j in range(2):
            kvb[kv * 18, j * 128 : (j + 1) * 128, :] = jnp.transpose(
                jnp.concatenate([keys_t[kv][j], keys_t[kv][j + 2]], axis=0)
            ).astype(BF16)

    def packet(h, src, dst, sem, seq_to):
        return pltpu.make_async_remote_copy(
            src_ref=kvb.at[18 * h + src],
            dst_ref=kvb.at[18 * h + dst],
            send_sem=kv_ssem.at[17 * h + sem],
            recv_sem=kv_rsem.at[18 * h + dst],
            device_id={"seq": seq_to, "tp": tp},
            device_id_type=MESH,
        )

    a1 = jnp.where(zh == 1, 9, 17)
    b1 = jnp.where(zh == 1, 17, 9)
    z_to = me + 2 - 4 * zh
    y_to = lax.rem(me + 16, n_seq)
    sib = me + 1 - 2 * core

    def x_to(j):
        return slab + lax.rem(me - slab + 16 - 4 * j, 16)

    def x_src(j, a, b):
        dest_x = lax.rem(xx + 4 - j, 4)
        return jnp.where(dest_x > xx, a, b)

    def copy_z(h):
        return packet(h, 0, jnp.where(zh == 0, 9, 17), 0, z_to)

    def copy_y0(h):
        return packet(h, 0, 1, 1, y_to)

    def copy_y1(h):
        return packet(h, a1, b1, 2, y_to)

    def copies_x0(h):
        return [packet(h, x_src(j, 0, 1), 2 + j, 2 + j, x_to(j)) for j in (1, 2, 3)]

    def copies_x1(h):
        return [packet(h, x_src(j, a1, b1), 10 + j, 5 + j, x_to(j)) for j in (1, 2, 3)]

    def copy_c0(h):
        return packet(h, jnp.where(core == 0, 0, 1), 2, 9, sib)

    def copy_c1(h):
        return packet(h, 9, 10, 10, sib)

    def copies_f0(h):
        return [packet(h, 2 + j, 5 + j, 10 + j, sib) for j in (1, 2, 3)]

    def copies_f1(h):
        return [packet(h, 10 + j, 13 + j, 13 + j, sib) for j in (1, 2, 3)]

    def arrived(h, slot):
        here_at = kvb.at[18 * h + slot]
        pltpu.make_async_copy(here_at, here_at, kv_rsem.at[18 * h + slot]).wait()

    for h in range(2):
        copy_y0(h).start()
        copy_z(h).start()
    for copy in weights_z:
        copy.wait_recv()
    for copy in weights_x:
        copy.start()

    def values_of(h, slot, half):
        at = 256 + half * 160
        return jnp.concatenate(
            [kvb[18 * h + slot, at : at + 80, :], kvb[18 * h + slot, at + 80 : at + 160, :]], axis=1
        )

    for c in range(CHUNKS):
        span = (c + 1) * 128
        key_at = lax.broadcasted_iota(jnp.int32, (span, 128), 0).astype(F32)
        query_at = lax.broadcasted_iota(jnp.int32, (span, 128), 1).astype(F32) + c * 128
        allowed1 = (key_at <= query_at) & (key_at >= first[:, c * 128 : (c + 1) * 128])
        bias1 = jnp.where(allowed1, 0.0, -BIG)
        bias = jnp.concatenate([bias1, bias1, bias1, bias1], axis=1)
        for kv in range(2):
            lanes = slice(kv * 2048 + c * 512, kv * 2048 + c * 512 + 512)
            parts = [
                jnp.dot(
                    kvb[18 * kv, 0 : min(span, 256), :],
                    qt[0, 0:128, lanes],
                    preferred_element_type=F32,
                )
            ]
            vals = [values_of(kv, 0, 0)]
            if span > 256:
                parts.append(
                    jnp.dot(
                        kvb[18 * kv, 0 : span - 256, :],
                        qt[1, 0:128, lanes],
                        preferred_element_type=F32,
                    )
                )
                vals.append(values_of(kv, 0, 1))
            s = jnp.concatenate(parts, axis=0) + bias
            top = jnp.max(s, axis=0, keepdims=True)
            p = jnp.exp2(s - top).astype(BF16)
            mx[:, lanes] = jnp.broadcast_to(top, (8, 512))
            acc[:, lanes] = jnp.dot(
                jnp.concatenate(vals, axis=1)[:, 0:span], p, preferred_element_type=F32
            )

    u_at = lax.broadcasted_iota(jnp.int32, (512, 128), 0).astype(F32)
    f_lane = lax.broadcasted_iota(jnp.int32, (512, 128), 1)

    def prepare(slot):
        strange = jnp.zeros((1, 128), F32)
        for j in range(4):
            aux = kvb[slot, 256 + j * 80 + 64 : 256 + j * 80 + 80, :].astype(F32)
            strange = strange + jnp.where(aux[1:2, :] != seg0, 1.0, 0.0)
        count = jnp.sum(strange, axis=1, keepdims=True)
        bias = jnp.where(u_at < count, -BIG, 0.0)
        kf[slot] = jnp.where(f_lane == 0, 1.0, jnp.where(f_lane == 1, bias, 0.0)).astype(BF16)

    def unit(slot, h, start, width):
        lanes = pl.ds(start, width)
        scores, vals = [], []
        for half in range(2):
            k = jnp.concatenate(
                [
                    jnp.concatenate(
                        [kvb[18 * h + s, 0:256, :], kf[s, half * 256 : half * 256 + 256, :]], axis=1
                    )
                    for s in (slot, slot + 1)
                ],
                axis=0,
            )
            scores.append(jnp.dot(k, qt[half, :, lanes], preferred_element_type=F32))
            vals.append(
                jnp.concatenate([values_of(h, slot, half), values_of(h, slot + 1, half)], axis=1)
            )
        old = mx[:, lanes]
        tops = [jnp.max(s, axis=0, keepdims=True) for s in scores]
        new = jnp.maximum(old, jnp.maximum(tops[0], tops[1]))
        factor = jnp.exp2(old - new)
        total = acc[:, lanes] * factor[0:1]
        for s, v in zip(scores, vals):
            p = jnp.exp2(s - new[0:1]).astype(BF16)
            total = total + jnp.dot(v, p, preferred_element_type=F32)
        acc[:, lanes] = total
        mx[:, lanes] = new

    def spread(h):
        arrived(h, 1)
        for copy in copies_x0(h):
            copy.start()
        copy_c0(h).start()

    def spread_y(h):
        arrived(h, a1)
        copy_y1(h).start()

    def spread_late(h):
        arrived(h, b1)
        for copy in copies_x1(h):
            copy.start()
        copy_c1(h).start()

    def attended_copy(piece, k):
        return pltpu.make_async_remote_copy(
            src_ref=att.at[piece],
            dst_ref=att_in.at[piece, k - 1],
            send_sem=r_ssem.at[piece, k - 1],
            recv_sem=r_rsem.at[piece, k - 1],
            device_id={"seq": me, "tp": lax.rem(tp + k, n_tp)},
            device_id_type=MESH,
        )

    def conclude(h, c):
        a = acc[:, pl.ds(pl.multiple_of(h * 2048 + c * 512, 512), 512)]
        o = a[0:64] / a[64:65]
        for pair in range(2):
            two = jnp.concatenate(
                [o[:, pair * 256 : pair * 256 + 128], o[:, pair * 256 + 128 : pair * 256 + 256]],
                axis=0,
            )
            att[h * 4 + c, :, pair * 128 : pair * 128 + 128] = jnp.transpose(two).astype(BF16)
        for k in (2, 3, 1):
            attended_copy(h * 4 + c, k).start()

    def arrive0(i):
        @pl.when(i == 0)
        def _():
            spread(0)

        @pl.when(i == 1)
        def _():
            spread(1)
            spread_y(0)

        @pl.when(i == 2)
        def _():
            spread_late(0)
            for copy in weights_x:
                copy.wait_recv()
            for copy in weights_y:
                copy.start()

        @pl.when(i == 3)
        def _():
            spread_y(1)

        @pl.when(i == 4)
        def _():
            for slot in (3, 4, 5):
                arrived(1, slot)
            for copy in copies_f0(1):
                copy.start()

        @pl.when(i == 5)
        def _():
            spread_late(1)

        for j in range(2):
            slot = 2 * i + 1 + j

            @pl.when((slot != 1) & (slot != 9))
            def _():
                arrived(0, slot)

            @pl.when(((slot >= 3) & (slot <= 5)) | ((slot >= 11) & (slot <= 13)))
            def _():
                wave = jnp.where(slot >= 11, 1, 0)
                packet(0, slot, slot + 3, slot + 8 - 5 * wave, sib).start()

            prepare(slot)

        @pl.when((i >= 3) & (i <= 6))
        def _():
            at = 32 + CACHE_AHEAD + (i - 3) * CACHE_STEP
            lax.fori_loop(at, at + CACHE_STEP, cache_start, 0)

    def early0(i, carry):
        arrive0(i)
        unit(2 * i + 1, 0, 0, 2048)
        return carry

    lax.fori_loop(0, EARLY_PAIRS[0], early0, 0)

    def late0(c, carry):
        def step(i, inner):
            @pl.when(c == 0)
            def _():
                arrive0(i)

            unit(2 * i + 1, 0, pl.multiple_of(c * 512, 512), 512)
            return inner

        lax.fori_loop(EARLY_PAIRS[0], PAIRS, step, 0)
        conclude(0, c)
        return carry

    lax.fori_loop(0, CHUNKS, late0, 0)

    def arrive1(i):
        @pl.when(i == 0)
        def _():
            for copy in weights_y:
                copy.wait_recv()
            weight_c.start()

        @pl.when(i == 1)
        def _():
            for slot in (11, 12, 13):
                arrived(1, slot)
            for copy in copies_f1(1):
                copy.start()

        for j in range(2):
            slot = 2 * i + 1 + j

            @pl.when(
                (slot == 2)
                | (slot == 10)
                | ((slot >= 6) & (slot <= 8))
                | ((slot >= 14) & (slot <= 16))
            )
            def _():
                arrived(1, slot)

    def early1(i, carry):
        arrive1(i)
        unit(2 * i + 1, 1, 2048, 2048)
        return carry

    lax.fori_loop(0, EARLY_PAIRS[1], early1, 0)

    def square_copy(c, k):
        return pltpu.make_async_remote_copy(
            src_ref=ss_send.at[c],
            dst_ref=ss_recv.at[c, k - 1],
            send_sem=s_ssem.at[c, k - 1],
            recv_sem=s_rsem.at[c, k - 1],
            device_id={"seq": me, "tp": lax.rem(tp + k, n_tp)},
            device_id_type=MESH,
        )

    own_col = pl.ds(pl.multiple_of(tp * 512, 512), 512)

    def weight_of(k, h):
        if k == 0:
            return wov[h * 256 : h * 256 + 256, own_col]
        return jnp.concatenate([wg[h * 16 + e, k - 1] for e in range(16)], axis=0)

    def first_half():
        for k in range(1, n_tp):
            for c in range(CHUNKS):
                attended_copy(c, k).wait_recv()
        weight_c.wait_recv()
        total = xv[:, own_col].astype(F32)
        for k in range(n_tp):
            a = jnp.concatenate(
                [att[c] if k == 0 else att_in[c, k - 1] for c in range(CHUNKS)], axis=0
            )
            total = total + jnp.dot(a, weight_of(k, 0), preferred_element_type=F32)
        resid[...] = total

    def settle(c):
        rows = pl.ds(pl.multiple_of(c * 128, 128), 128)
        total = resid[rows, :]
        for k in range(n_tp):
            if k > 0:
                attended_copy(4 + c, k).wait_recv()
            a = att[4 + c] if k == 0 else att_in[4 + c, k - 1]
            total = total + jnp.dot(a, weight_of(k, 1), preferred_element_type=F32)
        resid[rows, :] = total
        hid_ref[rows, :] = total.astype(BF16)
        square = jnp.sum(total * total, axis=1, keepdims=True)
        ss_send[c] = jnp.transpose(jnp.broadcast_to(square, (128, 128)))[0:8]
        for k in range(1, n_tp):
            square_copy(c, k).start()

    def late(c, carry):
        def step(i, inner):
            @pl.when(c == 0)
            def _():
                arrive1(i)

            unit(2 * i + 1, 1, pl.multiple_of(2048 + c * 512, 512), 512)
            return inner

        lax.fori_loop(EARLY_PAIRS[1], PAIRS, step, 0)
        conclude(1, c)

        @pl.when(c == 1)
        def _():
            first_half()

        @pl.when(c > 0)
        def _():
            settle(c - 1)

        return carry

    lax.fori_loop(0, CHUNKS, late, 0)
    settle(CHUNKS - 1)

    def finish(c, carry):
        rows = pl.ds(pl.multiple_of(c * 128, 128), 128)
        square = ss_send[c]
        for k in range(1, n_tp):
            square_copy(c, k).wait_recv()
            square = square + ss_recv[c, k - 1]
        column = jnp.transpose(jnp.broadcast_to(square[0:1], (128, 128)))
        scale = lax.rsqrt(column[:, 0:1] * (1.0 / 2048.0) + 1e-05)
        mlp_ref[rows, :] = (resid[rows, :] * scale * ogain_ref[...]).astype(BF16)
        for k in range(1, n_tp):
            attended_copy(c, k).wait_send()
            attended_copy(4 + c, k).wait_send()
            square_copy(c, k).wait_send()
        return carry

    lax.fori_loop(0, CHUNKS, finish, 0)

    for h in range(2):
        for copy in [copy_z(h), copy_y0(h), copy_y1(h), copy_c0(h), copy_c1(h)]:
            copy.wait_send()
        for copy in copies_x0(h) + copies_x1(h) + copies_f0(h) + copies_f1(h):
            copy.wait_send()
    for copy in weights_z + weights_x + weights_y + [weight_c]:
        copy.wait_send()

    def cache_wait(k, carry):
        cache_copy(k).wait_send()
        cache_copy(k).wait_recv()
        return carry

    lax.fori_loop(1, n_seq, cache_wait, 0)
    cp_own.wait()


def hand_over(hid, mlp, dec, hid_out, mlp_out, dec_out, hid_v, mlp_v, dec_v, in_sems, out_sems):
    pieces = [(hid, hid_v, hid_out), (mlp, mlp_v, mlp_out)]
    step = dec.shape[0] // 4
    for k in range(4):
        rows = pl.ds(step * k, step)
        pieces.append((dec.at[rows], dec_v.at[rows], dec_out.at[rows]))
    ins = [pltpu.make_async_copy(a, v, in_sems.at[k]) for k, (a, v, b) in enumerate(pieces)]
    outs = [pltpu.make_async_copy(v, b, out_sems.at[k]) for k, (a, v, b) in enumerate(pieces)]
    for copy in ins:
        copy.start()
    for first, second in zip(ins, outs):
        first.wait()
        second.start()
    for copy in outs:
        copy.wait()


def per_device(
    n_seq,
    n_tp,
    tokens,
    norm_gain,
    query_key_value_weight,
    output_weight,
    out_gain,
    seg_ids,
    earlier_cache,
    decode_owner,
):
    tok, width = tokens.shape
    blocks = earlier_cache.shape[0]
    w = query_key_value_weight.reshape(width, -1)
    wo = output_weight.reshape(-1, width)
    owner = decode_owner[:, 0]
    index = jnp.arange(blocks, dtype=jnp.int32)
    same = (owner[:, None] == owner[None, :]) & (index[:, None] < index[None, :])
    slot = owner * 2 + jnp.sum(same.astype(jnp.int32), axis=0)
    hit = slot[None, :] == jnp.arange(2 * n_seq, dtype=jnp.int32)[:, None]
    inverse = jnp.min(jnp.where(hit, index[None, :], blocks), axis=1)
    rope = jnp.asarray(rope_tables(tok, n_seq))
    share = width // n_tp
    vmem = pl.BlockSpec(memory_space=pltpu.VMEM)
    hbm = pl.BlockSpec(memory_space=pl.ANY)
    smem = pl.BlockSpec(memory_space=pltpu.SMEM)
    dma = pltpu.SemaphoreType.DMA
    hidden, mlp, dec = pl.pallas_call(
        functools.partial(body, n_seq, n_tp),
        out_shape=(
            jax.ShapeDtypeStruct((tok, share), BF16),
            jax.ShapeDtypeStruct((tok, share), BF16),
            jax.ShapeDtypeStruct((2 * n_seq, 2, 2048), BF16),
        ),
        in_specs=[hbm, vmem, hbm, hbm, vmem, vmem, hbm, smem, vmem],
        out_specs=(vmem, vmem, hbm),
        scratch_shapes=[
            pltpu.VMEM((tok, width), BF16),
            pltpu.VMEM((width, 768), BF16),
            pltpu.VMEM((512, width), BF16),
            pltpu.VMEM((blocks + 1, 2, 2048), BF16),
            pltpu.VMEM((2 * n_seq, 2, 2048), BF16),
            pltpu.VMEM((36, PACKET_ROWS, 128), BF16),
            pltpu.VMEM((18, 512, 128), BF16),
            pltpu.VMEM((2, 256, 4096), BF16),
            pltpu.VMEM((8, 4096), F32),
            pltpu.VMEM((80, 4096), F32),
            pltpu.VMEM((tok, share), F32),
            pltpu.VMEM((2 * CHUNKS, 128, 256), BF16),
            pltpu.VMEM((2 * CHUNKS, 3, 128, 256), BF16),
            pltpu.VMEM((32, 3, 16, share), BF16),
            pltpu.VMEM((CHUNKS, 8, 128), F32),
            pltpu.VMEM((CHUNKS, 3, 8, 128), F32),
            dma((5,)),
            dma((64,)),
            dma((64,)),
            dma((34,)),
            dma((36,)),
            dma((2 * CHUNKS, 3)),
            dma((2 * CHUNKS, 3)),
            dma((CHUNKS, 3)),
            dma((CHUNKS, 3)),
            dma((10,)),
            dma((10,)),
        ],
        compiler_params=pltpu.CompilerParams(
            collective_id=0, has_side_effects=True, vmem_limit_bytes=58 << 20
        ),
        name="attention_block",
    )(
        tokens,
        norm_gain.reshape(1, -1),
        w,
        wo,
        out_gain.reshape(1, -1),
        seg_ids.reshape(1, -1),
        earlier_cache,
        inverse,
        rope,
    )
    return pl.pallas_call(
        hand_over,
        out_shape=(
            jax.ShapeDtypeStruct((tok, share), BF16),
            jax.ShapeDtypeStruct((tok, share), BF16),
            jax.ShapeDtypeStruct((2 * n_seq, 2, 2048), BF16),
        ),
        in_specs=[hbm, hbm, hbm],
        out_specs=(hbm, hbm, hbm),
        scratch_shapes=[
            pltpu.VMEM((tok, share), BF16),
            pltpu.VMEM((tok, share), BF16),
            pltpu.VMEM((2 * n_seq, 2, 2048), BF16),
            dma((6,)),
            dma((6,)),
        ],
        name="hand_over",
    )(hidden, mlp, dec)


def solution(mesh):
    n_seq, n_tp = mesh.shape["seq"], mesh.shape["tp"]
    in_specs = (
        P("seq", None),
        P(),
        P(None, "tp", None),
        P("tp", None, None),
        P("tp"),
        P("seq"),
        P("seq", "tp", None),
        P("seq", None),
    )
    out_specs = (P("seq", "tp"), P("seq", "tp"), P("seq", "tp", None))
    return jax.shard_map(
        functools.partial(per_device, n_seq, n_tp),
        mesh=mesh,
        in_specs=in_specs,
        out_specs=out_specs,
        check_vma=False,
    )
```
